512 devices in a mesh: row: 16 (over x, y), col: 32 (over z, core).
Axes of the slice: x: 4, y: 4, z: 16, core: 2. Of those that a mesh axis runs over, the one named last changes fastest.
Arguments:
- positions: float32 [3, 32768], P(None, ('row', 'col')), may hold values from -1 to 96, as said below
- noise: float32 [8, 3, 32768], P(None, None, ('row', 'col')), may hold values from -6 to 6
Outputs:
- basis: float32 [8, 3, 32768], P(None, None, ('row', 'col'))
- residual: float32 [8, 3, 32768], P(None, None, ('row', 'col'))
- coefficients: float32 [3, 8, 8], replicated
The draws below stay inside these ranges and needn't reach their ends.
Inputs may be any that keep to these rules, and one draw needn't show every extreme that they name: `positions`: bead k lies within 0.77 of each coordinate of its own point of a cubic lattice of spacing 2.2 with 32 by 32 points a layer, distinct beads on distinct points.
All inputs are finite; a program needn't handle non-finite values.
Results may differ from the reference program's by a relative error of at most 0.0003.
Values sent between devices are 32-bit elements; how exact they have to be, the bound alone decides.
A program may use at most 64 MiB of HBM per device.

```python
import jax
import jax.numpy as jnp
from jax import lax

VECS = 8
BEADS = 32768


def draw_positions(key, part):
    order_key = jax.random.fold_in(key, 11)
    jitter_key = jax.random.fold_in(key, 12)
    sites = jax.random.permutation(order_key, BEADS)
    lattice = jnp.stack([sites % 32, sites // 32 % 32, sites // 1024]).astype(jnp.float32)
    jitter_reach = 0.22
    jitter = jax.random.uniform(jitter_key, (3, BEADS), jnp.float32, -jitter_reach, jitter_reach)
    return 2.2 * (lattice + jitter)


def block_levels(stream_key, dims, cuts, low, top_value):
    factor_of, own = 1.0, jax.random.fold_in(stream_key, 6)
    for axis_at, parts in cuts:
        steps = jnp.exp(jax.random.uniform(jax.random.fold_in(own, axis_at), (parts,), jnp.float32, low / len(cuts), top_value / len(cuts)))
        factor_of = factor_of * jnp.repeat(steps, dims[axis_at] // parts).reshape([-1 if axis == axis_at else 1 for axis in range(len(dims))])
    return factor_of


def gaussian(rng, extent, width, most, pieces=(), kind=jnp.bfloat16):
    values = jax.random.normal(rng, extent, jnp.float32) * width
    if len(pieces) > 0:
        values = block_levels(rng, extent, pieces, -0.22, 0.18) * values
    return jnp.clip(values, min=-most, max=most).astype(kind)


def setup_inputs(seed: int = 0) -> dict:
    seeds = jax.random.split(jax.random.key(seed), 3)
    return {
        "positions": draw_positions(jax.random.fold_in(seeds[2], 71), 0),
        "noise": gaussian(seeds[1], (VECS, 3, BEADS), 1.0, 6.0, ((2, 512),), jnp.float32),
    }


def pair_tensor(target_pos, source_pos):
    displace = target_pos[:, :, None] - source_pos[:, None, :]
    distance_sq = lax.optimization_barrier(jnp.sum(displace * displace, axis=0))
    distance = jnp.sqrt(distance_sq)
    safe_distance = jnp.where(distance > 0, distance, 1.0)
    safe_sq = safe_distance * safe_distance
    far_iso = 0.75 / safe_distance * (1.0 + 2.0 / (3.0 * safe_sq))
    far_dir = 0.75 / safe_distance * (1.0 - 2.0 / safe_sq) / safe_sq
    near_iso = 1.0 - 9.0 * distance / 32.0
    near_dir = 3.0 / (32.0 * safe_distance)
    intersecting = distance < 2.0
    iso_part = jnp.where(intersecting, near_iso, far_iso)
    dir_part = jnp.where(intersecting, near_dir, far_dir)
    identity = jnp.eye(3, dtype=displace.dtype)
    return identity[:, :, None, None] * iso_part + dir_part * displace[:, None] * displace[None, :]

def apply_mobility(positions, vectors):
    total = positions.shape[1]
    blocks = positions.reshape(3, total // 32, 32).transpose(1, 0, 2)

    def one_block(target_pos):
        tensor = pair_tensor(target_pos, positions)
        return jnp.einsum('abts,kbs->kat', tensor, vectors, precision=lax.Precision.HIGHEST)
    images = lax.map(one_block, blocks)
    return images.transpose(1, 2, 0, 3).reshape(vectors.shape[0], 3, total)

def gram(left, right):
    return jnp.einsum('kan,jan->kj', left, right, precision=lax.Precision.HIGHEST) / (3.0 * left.shape[2])

def combine(vectors, matrix):
    return jnp.einsum('kan,kj->jan', vectors, matrix, precision=lax.Precision.HIGHEST)

def orthonormal(block):
    factor = jnp.linalg.cholesky(gram(block, block))
    inverse = jax.scipy.linalg.solve_triangular(factor, jnp.eye(factor.shape[0], dtype=factor.dtype), lower=True)
    return (combine(block, inverse.T), factor)

def reference(positions, noise):
    first, unused_factor = orthonormal(noise)
    image = apply_mobility(positions, first)
    alpha_one = gram(first, image)
    remainder = image - combine(first, alpha_one)
    basis, factor_one = orthonormal(remainder)
    image = apply_mobility(positions, basis) - combine(first, factor_one)
    alpha_two = gram(basis, image)
    residual = image - combine(basis, alpha_two)
    return (basis, residual, jnp.stack([alpha_one, factor_one, alpha_two]))
```

```python
import jax
import jax.numpy as jnp
from jax import lax
from jax.experimental import pallas as pl
from jax.experimental.pallas import tpu as pltpu
from jax.sharding import PartitionSpec as P

F32 = jnp.float32
BF16 = jnp.bfloat16
MESH = pl.DeviceIdType.MESH
HIGHEST = lax.Precision.HIGHEST
NT = (((1,), (1,)), ((), ()))
NN = (((1,), (0,)), ((), ()))
TN = (((0,), (0,)), ((), ()))

COLS = 16
PLANE = 32
WIDTH = 64
NCOL = COLS * WIDTH
NPLANE = PLANE * WIDTH
CENTRE = 34.1
CHUNK = 256
BEADS = 32768


def dot(left, right, dims):
    return lax.dot_general(left, right, dims, preferred_element_type=F32)


def exact_dot(left, right, dims):
    return lax.dot_general(left, right, dims, precision=HIGHEST, preferred_element_type=F32)


def split(value):
    high = value.astype(BF16)
    return high, (value - high.astype(F32)).astype(BF16)


def pair_strip(col_pos, plane_pos):
    shift = [c - p for c, p in zip(col_pos, plane_pos)]
    square = jnp.maximum(shift[0] * shift[0] + shift[1] * shift[1] + shift[2] * shift[2], 1e-12)
    inv = lax.rsqrt(square)
    inv2 = inv * inv
    inv3 = inv * inv2
    near = square < 4.0
    iso = jnp.where(near, 1.0 - (9.0 / 32.0) * (square * inv), 0.75 * inv + 0.5 * inv3)
    along = jnp.where(near, (3.0 / 32.0) * inv, inv3 * (0.75 - 1.5 * inv2))
    return [iso] + [along * s for s in shift]


def lower_factor(matrix):
    row = lax.broadcasted_iota(jnp.int32, (8, 8), 0)
    col = lax.broadcasted_iota(jnp.int32, (8, 8), 1)
    left = matrix
    right = jnp.where(row == col, 1.0, 0.0).astype(F32)
    for j in range(8):
        pivot = 1.0 / left[j : j + 1, j : j + 1]
        ratio = jnp.where(row[:, :1] > j, left[:, j : j + 1] * pivot, 0.0)
        left, right = left - ratio * left[j : j + 1, :], right - ratio * right[j : j + 1, :]
    diagonal = jnp.sum(jnp.where(row == col, left, 0.0), axis=1, keepdims=True)
    scale = lax.rsqrt(diagonal)
    scale = scale * (1.5 - 0.5 * diagonal * scale * scale)
    upper = jnp.where(col >= row, left * scale, 0.0)
    return upper, right * scale


def kernel(
    pos_ref, noise_ref, basis_ref, resid_ref, coef_ref,
    col_pos, col_vec, plane_pos, send1, got1, own_y, plane_vec, send2, got2, gram1, gram2, all1, all2,
    wide, col_row, plane_row, xs, ys, high, low, sent, came,
):
    row = lax.axis_index("row")
    col = lax.axis_index("col")
    x, y, z, core = row // 4, row % 4, col // 2, col % 2

    def plane_peer(j):
        dx, dy, dc = j // 8, j // 2 % 4, j % 2
        there = {"row": (x + dx) % 4 * 4 + (y + dy) % 4, "col": z * 2 + (core + dc) % 2}
        back = ((4 - dx) % 4 * 4 + (4 - dy) % 4) * 2 + dc
        return there, back

    def col_peer(t):
        return {"row": row, "col": (z + t) % 16 * 2 + core}, (16 - t) % 16

    def copy(kind, source, target, slot, back, there):
        return pltpu.make_async_remote_copy(
            src_ref=source, dst_ref=target.at[back], send_sem=sent.at[kind, slot], recv_sem=came.at[kind, back],
            device_id=there, device_id_type=MESH,
        )

    def to_plane(kind, source, target):
        def send(j, carry):
            there, back = plane_peer(j)
            copy(kind, source(j), target, j, back, there).start()
            return carry
        lax.fori_loop(1, PLANE, send, 0)

    def to_col(kind, source, target):
        def send(t, carry):
            there, back = col_peer(t)
            copy(kind, source(t), target, t, back, there).start()
            return carry
        lax.fori_loop(1, COLS, send, 0)

    def arrived(kind, source, target, slot):
        here = {"row": row, "col": col}
        pltpu.make_async_remote_copy(
            src_ref=source, dst_ref=target.at[slot], send_sem=sent.at[kind, slot], recv_sem=came.at[kind, slot],
            device_id=here, device_id_type=MESH,
        ).wait_recv()

    def left(kind, source, target, slot):
        here = {"row": row, "col": col}
        pltpu.make_async_remote_copy(
            src_ref=source, dst_ref=target.at[slot], send_sem=sent.at[kind, slot], recv_sem=came.at[kind, slot],
            device_id=here, device_id_type=MESH,
        ).wait_send()

    def wait_all(kind, source, target, count):
        def step(j, carry):
            arrived(kind, source, target, j)
            return carry
        lax.fori_loop(1, count, step, 0)

    barrier = pltpu.get_barrier_semaphore()

    def greet_plane(j, carry):
        there, back = plane_peer(j)
        pl.semaphore_signal(barrier, inc=1, device_id=there, device_id_type=MESH)
        return carry

    def greet_col(t, carry):
        there, back = col_peer(t)
        pl.semaphore_signal(barrier, inc=1, device_id=there, device_id_type=MESH)
        return carry

    lax.fori_loop(1, COLS, greet_col, 0)
    lax.fori_loop(1, PLANE, greet_plane, 0)
    pl.semaphore_wait(barrier, COLS + PLANE - 2)

    to_col(0, lambda t: pos_ref, col_pos)
    to_plane(2, lambda t: pos_ref, plane_pos)
    to_col(1, lambda t: noise_ref, col_vec)
    col_pos[0] = pos_ref[...]
    plane_pos[0] = pos_ref[...]
    col_vec[0] = noise_ref[...]

    wait_all(0, pos_ref, col_pos, COLS)
    wait_all(2, pos_ref, plane_pos, PLANE)

    for i in range(PLANE // 2):
        plane_row[:, 128 * i : 128 * i + 128] = jnp.concatenate([plane_pos[2 * i], plane_pos[2 * i + 1]], axis=1) - CENTRE
    for i in range(COLS // 2):
        col_row[:, 128 * i : 128 * i + 128] = jnp.concatenate([col_pos[2 * i], col_pos[2 * i + 1]], axis=1) - CENTRE
    equal = lax.broadcasted_iota(jnp.int32, (128, 128), 0) == lax.broadcasted_iota(jnp.int32, (128, 128), 1)

    def widen(i, carry):
        lanes = pl.ds(pl.multiple_of(i * 128, 128), 128)
        for a in range(3):
            spread = jnp.sum(jnp.where(equal, col_row[a : a + 1, lanes], 0.0), axis=1, keepdims=True)
            wide[a, lanes, :] = jnp.broadcast_to(spread, (128, 128))
        return carry

    lax.fori_loop(0, NCOL // 128, widen, 0)

    def rows_of(vec, pos):
        along = pos[0:1] * vec[0:8] + pos[1:2] * vec[8:16] + pos[2:3] * vec[16:24]
        return split(jnp.concatenate([vec, along], axis=0))

    def fill(store, vec, lanes, pos):
        top, rest = rows_of(vec, pos)
        store[0:32, lanes] = top
        store[32:64, lanes] = rest

    wait_all(1, noise_ref, col_vec, COLS)
    for i in range(COLS // 2):
        lanes = pl.ds(128 * i, 128)
        fill(xs, jnp.concatenate([col_vec[2 * i], col_vec[2 * i + 1]], axis=1), lanes, col_row[:, lanes])

    def chunk(step, carry):
        at = NPLANE // CHUNK - 1 - step
        lanes = pl.ds(pl.multiple_of(at * CHUNK, CHUNK), CHUNK)
        here = plane_row[:, lanes]
        plane = [jnp.broadcast_to(here[a : a + 1], (16, CHUNK)) for a in range(3)]

        def strip(s, inner):
            for k in range(2):
                rows = pl.ds(pl.multiple_of(s * 32 + k * 16, 16), 16)
                column = [jnp.concatenate([wide[a, rows, :]] * (CHUNK // 128), axis=1) for a in range(3)]
                for n, value in enumerate(pair_strip(column, plane)):
                    top, rest = split(value)
                    high[n, rows, lanes] = top
                    low[n, rows, lanes] = rest
            return inner

        lax.fori_loop(0, NCOL // 32, strip, 0)
        parts = []
        for n in range(4):
            both = dot(xs[...], high[n, :, lanes], NN)
            parts.append(both[0:32] + both[32:64] + dot(xs[0:32, :], low[n, :, lanes], NN))
        image = []
        for a in range(3):
            e = parts[1 + a]
            image.append(
                parts[0][8 * a : 8 * a + 8] + e[24:32]
                - here[0:1] * e[0:8] - here[1:2] * e[8:16] - here[2:3] * e[16:24]
            )
        image = jnp.concatenate(image, axis=0)
        for i in range(CHUNK // WIDTH):
            send1[at * (CHUNK // WIDTH) + i] = image[:, WIDTH * i : WIDTH * i + WIDTH]

        def send(i, inner):
            j = at * (CHUNK // WIDTH) + i

            @pl.when(j > 0)
            def _():
                there, back = plane_peer(j)
                copy(3, send1.at[j], got1, j, back, there).start()
            return inner

        lax.fori_loop(0, CHUNK // WIDTH, send, 0)
        return carry

    lax.fori_loop(0, NPLANE // CHUNK, chunk, 0)

    wait_all(3, send1.at[0], got1, PLANE)
    total = send1[0]
    for j in range(1, PLANE):
        total = total + got1[j]
    own_y[...] = total
    to_plane(4, lambda j: own_y, plane_vec)
    plane_vec[0] = total
    wait_all(4, own_y, plane_vec, PLANE)
    for i in range(PLANE // 2):
        lanes = pl.ds(128 * i, 128)
        fill(ys, jnp.concatenate([plane_vec[2 * i], plane_vec[2 * i + 1]], axis=1), lanes, plane_row[:, lanes])

    def tile(at, carry):
        rows = pl.ds(pl.multiple_of(at * CHUNK, CHUNK), CHUNK)
        here = col_row[:, rows]
        parts = []
        for n in range(4):
            both = dot(ys[...], high[n, rows, :], NT)
            parts.append(both[0:32] + both[32:64] + dot(ys[0:32, :], low[n, rows, :], NT))
        image = []
        for a in range(3):
            e = parts[1 + a]
            image.append(
                parts[0][8 * a : 8 * a + 8] - e[24:32]
                + here[0:1] * e[0:8] + here[1:2] * e[8:16] + here[2:3] * e[16:24]
            )
        image = jnp.concatenate(image, axis=0)
        for i in range(CHUNK // WIDTH):
            send2[at * (CHUNK // WIDTH) + i] = image[:, WIDTH * i : WIDTH * i + WIDTH]

        def send(i, inner):
            t = at * (CHUNK // WIDTH) + i

            @pl.when(t > 0)
            def _():
                there, back = col_peer(t)
                copy(5, send2.at[t], got2, t, back, there).start()
            return inner

        lax.fori_loop(0, CHUNK // WIDTH, send, 0)
        return carry

    lax.fori_loop(0, NCOL // CHUNK, tile, 0)

    wait_all(5, send2.at[0], got2, COLS)
    final = send2[0]
    for t in range(1, COLS):
        final = final + got2[t]

    vec_n, vec_y, vec_z = noise_ref[...], own_y[...], final
    gram = jnp.zeros((24, 24), F32)
    for a in range(3):
        part = slice(8 * a, 8 * a + 8)
        block = jnp.concatenate([vec_n[part], vec_y[part], vec_z[part]], axis=0)
        gram = gram + exact_dot(block, block, NT)
    gram1[...] = gram
    to_plane(6, lambda j: gram1, all1)
    wait_all(6, gram1, all1, PLANE)
    for j in range(1, PLANE):
        gram = gram + all1[j]
    gram2[...] = gram
    to_col(7, lambda j: gram2, all2)
    all2[0] = gram
    wait_all(7, gram2, all2, COLS)
    gram = all2[(16 - z) % 16]
    for t in range(1, COLS):
        gram = gram + all2[(t + 16 - z) % 16]
    gram = gram * (1.0 / (3.0 * BEADS))

    nn, ny, nz = gram[0:8, 0:8], gram[0:8, 8:16], gram[0:8, 16:24]
    yn, yy, yz = gram[8:16, 0:8], gram[8:16, 8:16], gram[8:16, 16:24]
    upper0, inv0 = lower_factor(nn)
    half = exact_dot(inv0, ny, NN)
    alpha1 = exact_dot(half, inv0, NT)
    image_gram = exact_dot(exact_dot(inv0, yy, NN), inv0, NT)
    upper1, inv1 = lower_factor(image_gram - exact_dot(alpha1, alpha1, TN))
    e_t = exact_dot(inv1, inv0, NN)
    f_t = exact_dot(inv1, exact_dot(alpha1, inv0, TN), NN)
    g_t = exact_dot(upper1, inv0, NN)
    y_w = exact_dot(yz, e_t, NT) - exact_dot(yy, f_t, NT) - exact_dot(yn, g_t, NT)
    n_w = exact_dot(nz, e_t, NT) - exact_dot(ny, f_t, NT) - exact_dot(nn, g_t, NT)
    alpha2 = exact_dot(e_t, y_w, NN) - exact_dot(f_t, n_w, NN)
    coef_ref[0] = alpha1
    coef_ref[1] = upper1.T
    coef_ref[2] = alpha2
    for a in range(3):
        part = slice(8 * a, 8 * a + 8)
        base = exact_dot(e_t, vec_y[part], NN) - exact_dot(f_t, vec_n[part], NN)
        image = exact_dot(e_t, vec_z[part], NN) - exact_dot(f_t, vec_y[part], NN) - exact_dot(g_t, vec_n[part], NN)
        basis_ref[:, a, :] = base
        resid_ref[:, a, :] = image - exact_dot(alpha2, base, TN)

    def drain_plane(j, carry):
        left(2, pos_ref, plane_pos, j)
        left(3, send1.at[0], got1, j)
        left(4, own_y, plane_vec, j)
        left(6, gram1, all1, j)
        return carry

    def drain_col(t, carry):
        left(0, pos_ref, col_pos, t)
        left(1, noise_ref, col_vec, t)
        left(5, send2.at[0], got2, t)
        left(7, gram2, all2, t)
        return carry

    lax.fori_loop(1, PLANE, drain_plane, 0)
    lax.fori_loop(1, COLS, drain_col, 0)


def local(positions, noise):
    vmem = pl.BlockSpec(memory_space=pltpu.VMEM)
    rows = noise.transpose(1, 0, 2).reshape(24, WIDTH)
    return pl.pallas_call(
        kernel,
        out_shape=(
            jax.ShapeDtypeStruct((8, 3, WIDTH), F32),
            jax.ShapeDtypeStruct((8, 3, WIDTH), F32),
            jax.ShapeDtypeStruct((3, 8, 8), F32),
        ),
        in_specs=[vmem, vmem],
        out_specs=(vmem, vmem, vmem),
        scratch_shapes=[
            pltpu.VMEM((COLS, 3, WIDTH), F32),
            pltpu.VMEM((COLS, 24, WIDTH), F32),
            pltpu.VMEM((PLANE, 3, WIDTH), F32),
            pltpu.VMEM((PLANE, 24, WIDTH), F32),
            pltpu.VMEM((PLANE, 24, WIDTH), F32),
            pltpu.VMEM((24, WIDTH), F32),
            pltpu.VMEM((PLANE, 24, WIDTH), F32),
            pltpu.VMEM((COLS, 24, WIDTH), F32),
            pltpu.VMEM((COLS, 24, WIDTH), F32),
            pltpu.VMEM((24, 24), F32),
            pltpu.VMEM((24, 24), F32),
            pltpu.VMEM((PLANE, 24, 24), F32),
            pltpu.VMEM((COLS, 24, 24), F32),
            pltpu.VMEM((3, NCOL, 128), F32),
            pltpu.VMEM((3, NCOL), F32),
            pltpu.VMEM((3, NPLANE), F32),
            pltpu.VMEM((64, NCOL), BF16),
            pltpu.VMEM((64, NPLANE), BF16),
            pltpu.VMEM((4, NCOL, NPLANE), BF16),
            pltpu.VMEM((4, NCOL, NPLANE), BF16),
            pltpu.SemaphoreType.DMA((8, PLANE)),
            pltpu.SemaphoreType.DMA((8, PLANE)),
        ],
        compiler_params=pltpu.CompilerParams(
            collective_id=0, has_side_effects=True, vmem_limit_bytes=60 * 1024 * 1024
        ),
    )(positions, rows)


def solution(mesh):
    return jax.shard_map(
        local,
        mesh=mesh,
        in_specs=(P(None, ("row", "col")), P(None, None, ("row", "col"))),
        out_specs=(P(None, None, ("row", "col")), P(None, None, ("row", "col")), P()),
        check_vma=False,
    )
```

```python
import jax
import jax.numpy as jnp
from jax import lax
from jax.experimental import pallas as pl
from jax.experimental.pallas import tpu as pltpu
from jax.sharding import PartitionSpec as P

F32 = jnp.float32
BF16 = jnp.bfloat16
MESH = pl.DeviceIdType.MESH
HIGHEST = lax.Precision.HIGHEST
NT = (((1,), (1,)), ((), ()))
NN = (((1,), (0,)), ((), ()))
TN = (((0,), (0,)), ((), ()))

COLS = 16
PLANE = 32
WIDTH = 64
NCOL = COLS * WIDTH
NPLANE = PLANE * WIDTH
CENTRE = 34.1
CHUNK = 256
BEADS = 32768


def dot(left, right, dims):
    return lax.dot_general(left, right, dims, preferred_element_type=F32)


def exact_dot(left, right, dims):
    return lax.dot_general(left, right, dims, precision=HIGHEST, preferred_element_type=F32)


def split(value):
    high = value.astype(BF16)
    return high, (value - high.astype(F32)).astype(BF16)


def pair_strip(col_pos, plane_pos):
    shift = [c - p for c, p in zip(col_pos, plane_pos)]
    square = jnp.maximum(shift[0] * shift[0] + shift[1] * shift[1] + shift[2] * shift[2], 1e-12)
    inv = lax.rsqrt(square)
    inv2 = inv * inv
    inv3 = inv * inv2
    near = square < 4.0
    iso = jnp.where(near, 1.0 - (9.0 / 32.0) * (square * inv), 0.75 * inv + 0.5 * inv3)
    along = jnp.where(near, (3.0 / 32.0) * inv, inv3 * (0.75 - 1.5 * inv2))
    return [iso] + [along * s for s in shift]


def lower_factor(matrix):
    row = lax.broadcasted_iota(jnp.int32, (8, 8), 0)
    col = lax.broadcasted_iota(jnp.int32, (8, 8), 1)
    left = matrix
    right = jnp.where(row == col, 1.0, 0.0).astype(F32)
    for j in range(8):
        pivot = 1.0 / left[j : j + 1, j : j + 1]
        ratio = jnp.where(row[:, :1] > j, left[:, j : j + 1] * pivot, 0.0)
        left, right = left - ratio * left[j : j + 1, :], right - ratio * right[j : j + 1, :]
    diagonal = jnp.sum(jnp.where(row == col, left, 0.0), axis=1, keepdims=True)
    scale = lax.rsqrt(diagonal)
    scale = scale * (1.5 - 0.5 * diagonal * scale * scale)
    upper = jnp.where(col >= row, left * scale, 0.0)
    return upper, right * scale


def kernel(
    pos_ref, noise_ref, basis_ref, resid_ref, coef_ref,
    col_pos, col_vec, plane_pos, send1, got1, own_y, plane_vec, send2, got2, col_y,
    gram1, gram2, all1, all2, cross1, cross2, all3, all4,
    wide, col_row, plane_row, xs, ys, pair, image2, sent, came,
):
    row = lax.axis_index("row")
    col = lax.axis_index("col")
    x, y, z, core = row >> 2, row & 3, col >> 1, col & 1
    here = (row, col)

    def plane_peer(j):
        dx, dy, dc = j >> 3, (j >> 1) & 3, j & 1
        there = (((x + dx) & 3) * 4 + ((y + dy) & 3), z * 2 + (core ^ dc))
        back = ((((4 - dx) & 3) * 4 + ((4 - dy) & 3)) << 1) + dc
        return there, back

    def col_peer(t):
        return (row, ((z + t) & 15) * 2 + core), (16 - t) & 15

    def near(target):
        return [(target, 1, 4), (target, 12, 4), (target, 5, 4), (target, 9, 3)]

    lands = near(col_pos) + near(col_vec) + [
        (plane_pos, 1, PLANE - 1),
        (got1, 1, PLANE - 1),
        (plane_vec, 1, PLANE - 1),
        (col_y, 1, COLS - 1),
        (got2, 1, COLS - 1),
        (all1, 1, PLANE - 1),
        (all2, 1, COLS - 1),
        (all3, 1, PLANE - 1),
        (all4, 1, COLS - 1),
    ]
    POS, VEC, PLACE, SUM1, IMAGE, COLY, SUM2, GRAM1, GRAM2, CROSS1, CROSS2 = 0, 4, 8, 9, 10, 11, 12, 13, 14, 15, 16

    def copy(kind, source, target, there):
        return pltpu.make_async_remote_copy(
            src_ref=source, dst_ref=target, send_sem=sent.at[kind], recv_sem=came.at[kind],
            device_id=there, device_id_type=MESH,
        )

    def whole(kind):
        target, first, count = lands[kind]
        block = target.at[pl.ds(first, count)]
        return copy(kind, block, block, here)

    def wait(*kinds):
        for kind in kinds:
            whole(kind).wait_recv()

    def to_plane(kind, source):
        for j in range(1, PLANE):
            there, back = plane_peer(j)
            copy(kind, source, lands[kind][0].at[back], there).start()

    def to_col(kind, source):
        for t in range(1, COLS):
            there, back = col_peer(t)
            copy(kind, source, lands[kind][0].at[back], there).start()

    def to_near(kind, source):
        for d in range(1, 5):
            for side, t in ((0, 16 - d), (1, d)):
                there, back = col_peer(t)
                copy(kind + side, source, lands[kind][0].at[back], there).start()

    def relay(kind):
        target = lands[kind][0]
        wait(kind)
        copy(kind + 2, target.at[pl.ds(1, 4)], target.at[pl.ds(5, 4)], col_peer(12)[0]).start()
        wait(kind + 1)
        copy(kind + 3, target.at[pl.ds(13, 3)], target.at[pl.ds(9, 3)], col_peer(4)[0]).start()

    def each(count, step, start=0):
        def body(j, carry):
            step(j)
            return carry
        lax.fori_loop(start, count, body, 0)

    barrier = pltpu.get_barrier_semaphore()
    for peer, slots in ((plane_peer, range(1, PLANE)), (col_peer, (1, 2, 3, 4, 12, 13, 14, 15))):
        for j in slots:
            pl.semaphore_signal(barrier, inc=1, device_id=peer(j)[0], device_id_type=MESH)
    pl.semaphore_wait(barrier, PLANE + 7)

    to_near(POS, pos_ref)
    to_plane(PLACE, pos_ref)
    to_near(VEC, noise_ref)
    col_pos[0] = pos_ref[...]
    plane_pos[0] = pos_ref[...]
    col_vec[0] = noise_ref[...]

    relay(POS)
    wait(PLACE)
    for i in range(PLANE // 2):
        plane_row[:, 128 * i : 128 * i + 128] = jnp.concatenate([plane_pos[2 * i], plane_pos[2 * i + 1]], axis=1) - CENTRE
    equal = lax.broadcasted_iota(jnp.int32, (128, 128), 0) == lax.broadcasted_iota(jnp.int32, (128, 128), 1)

    def lanes_of(at):
        return pl.ds(pl.multiple_of(at * CHUNK, CHUNK), CHUNK)

    def plane_of(at):
        here = plane_row[:, lanes_of(at)]
        return [jnp.broadcast_to(here[a : a + 1], (16, CHUNK)) for a in range(3)]

    def build(i, at, plane):
        for k in range(8):
            rows = pl.ds(pl.multiple_of(i * 128 + k * 16, 16), 16)
            column = [jnp.concatenate([wide[a, rows, :]] * (CHUNK // 128), axis=1) for a in range(3)]
            for n, value in enumerate(pair_strip(column, plane)):
                top, rest = split(value)
                pair[2 * n, rows, lanes_of(at)] = top
                pair[2 * n + 1, rows, lanes_of(at)] = rest

    last = NPLANE // CHUNK - 1

    def prepare(i):
        lanes = pl.ds(pl.multiple_of(i * 128, 128), 128)
        both = jnp.concatenate([col_pos[2 * i], col_pos[2 * i + 1]], axis=1) - CENTRE
        col_row[:, lanes] = both
        for a in range(3):
            spread = jnp.sum(jnp.where(equal, both[a : a + 1], 0.0), axis=1, keepdims=True)
            wide[a, lanes, :] = jnp.broadcast_to(spread, (128, 128))

    plane = plane_of(last)

    def first(k):
        i = k + (k >> 1) * 4
        prepare(i)
        build(i, last, plane)

    def second(k):
        prepare(k)
        build(k, last, plane)

    each(4, first)
    wait(POS + 2, POS + 3)
    each(6, second, 2)
    relay(VEC)

    def build_all(at):
        plane = plane_of(at)
        each(8, lambda i: build(i, at, plane))

    build_all(last - 1)

    def fill(store, vec, lanes, pos):
        along = pos[0:1] * vec[0:8] + pos[1:2] * vec[8:16] + pos[2:3] * vec[16:24]
        top, rest = split(jnp.concatenate([vec, along], axis=0))
        store[0:32, lanes] = top
        store[32:64, lanes] = rest

    wait(VEC + 2, VEC + 3)
    for i in range(COLS // 2):
        lanes = pl.ds(128 * i, 128)
        vec = jnp.concatenate([col_vec[2 * i], col_vec[2 * i + 1]], axis=1)
        fill(xs, vec, lanes, col_row[:, lanes])

    def pack(value, lane):
        x, y, z = (value[8 * a : 8 * a + 8, lane : lane + WIDTH] for a in range(3))
        return jnp.concatenate([x, y], axis=1), jnp.concatenate([z, jnp.zeros_like(z)], axis=1)

    def unpack(one, two):
        return jnp.concatenate([
            jnp.concatenate([one[0:8, 0:WIDTH], two[0:8, 0:WIDTH]], axis=1),
            jnp.concatenate([one[0:8, WIDTH:], two[0:8, WIDTH:]], axis=1),
            jnp.concatenate([one[8:16, 0:WIDTH], two[8:16, 0:WIDTH]], axis=1),
        ], axis=0)

    def finish(at):
        here = plane_row[:, lanes_of(at)]
        full = []
        for n in range(4):
            both = dot(xs[...], pair[2 * n, :, lanes_of(at)], NN)
            full.append(both[0:32] + both[32:64] + dot(xs[0:32, :], pair[2 * n + 1, :, lanes_of(at)], NN))
        image = []
        for a in range(3):
            e = full[1 + a]
            image.append(
                full[0][8 * a : 8 * a + 8] + e[24:32]
                - here[0:1] * e[0:8] - here[1:2] * e[8:16] - here[2:3] * e[16:24]
            )
        image = jnp.concatenate(image, axis=0)
        for i in range(CHUNK // WIDTH):
            top, rest = pack(image, WIDTH * i)
            send1[at * (CHUNK // WIDTH) + i, 0:8] = top
            send1[at * (CHUNK // WIDTH) + i, 8:16] = rest

        for i in range(CHUNK // WIDTH):
            j = at * (CHUNK // WIDTH) + i

            @pl.when(j > 0)
            def _():
                there, back = plane_peer(j)
                copy(SUM1, send1.at[j], got1.at[back], there).start()

    finish(last)
    finish(last - 1)

    def chunk(step):
        at = last - step
        build_all(at)
        finish(at)

    each(NPLANE // CHUNK, chunk, 2)

    wait(SUM1)
    total = send1[0]
    for j in range(1, PLANE):
        total = total + got1[j]
    own_y[...] = total
    to_plane(IMAGE, own_y)
    to_col(COLY, own_y)
    plane_vec[0] = total
    col_y[0] = total

    def side(value):
        return jnp.concatenate([value[0:8], value[8:16, 0:WIDTH]], axis=1)

    vec_n = noise_ref[...]
    wide_n = jnp.concatenate([vec_n[0:8], vec_n[8:16], vec_n[16:24]], axis=1)
    wide_y = side(total)
    block = jnp.concatenate([wide_n, wide_y], axis=0)
    gram = exact_dot(block, block, NT)
    gram1[...] = gram
    to_plane(GRAM1, gram1)
    all1[0] = gram

    wait(IMAGE)
    for i in range(PLANE // 2):
        lanes = pl.ds(128 * i, 128)
        fill(ys, unpack(plane_vec[2 * i], plane_vec[2 * i + 1]), lanes, plane_row[:, lanes])

    def tile(at):
        rows = lanes_of(at)
        here = col_row[:, rows]
        full = []
        for n in range(4):
            both = dot(ys[...], pair[2 * n, rows, :], NT)
            full.append(both[0:32] + both[32:64])
        image = []
        for a in range(3):
            e = full[1 + a]
            image.append(
                full[0][8 * a : 8 * a + 8] - e[24:32]
                + here[0:1] * e[0:8] + here[1:2] * e[8:16] + here[2:3] * e[16:24]
            )
        image = jnp.concatenate(image, axis=0)
        image2[:, rows] = image
        for i in range(CHUNK // WIDTH):
            top, rest = pack(image, WIDTH * i)
            send2[at * (CHUNK // WIDTH) + i, 0:8] = top
            send2[at * (CHUNK // WIDTH) + i, 8:16] = rest

        for i in range(CHUNK // WIDTH):
            t = at * (CHUNK // WIDTH) + i

            @pl.when(t > 0)
            def _():
                there, back = col_peer(t)
                copy(SUM2, send2.at[t], got2.at[back], there).start()

    each(NCOL // CHUNK, tile)

    wait(COLY)
    cross = jnp.zeros((8, 8), F32)
    y_rows = jnp.concatenate([unpack(col_y[t], col_y[t + 1]) for t in range(0, COLS, 2)], axis=1)
    for a in range(3):
        part = slice(8 * a, 8 * a + 8)
        cross = cross + exact_dot(y_rows[part], image2[part, :], NT)
    cross1[...] = cross
    to_plane(CROSS1, cross1)
    all3[0] = cross

    wait(GRAM1)
    for j in range(1, PLANE):
        gram = gram + all1[j]
    gram2[...] = gram
    to_col(GRAM2, gram2)
    all2[0] = gram

    wait(CROSS1)
    for j in range(1, PLANE):
        cross = cross + all3[j]
    cross2[...] = cross
    to_col(CROSS2, cross2)
    all4[0] = cross

    def planes(store):
        value = store[(16 - z) % 16]
        for t in range(1, COLS):
            value = value + store[(t + 16 - z) % 16]
        return value * (1.0 / (3.0 * BEADS))

    wait(GRAM2)
    gram = planes(all2)
    nn, ny, yn, yy = gram[0:8, 0:8], gram[0:8, 8:16], gram[8:16, 0:8], gram[8:16, 8:16]
    upper0, inv0 = lower_factor(nn)
    alpha1 = exact_dot(exact_dot(inv0, ny, NN), inv0, NT)
    image_gram = exact_dot(exact_dot(inv0, yy, NN), inv0, NT)
    upper1, inv1 = lower_factor(image_gram - exact_dot(alpha1, alpha1, TN))
    e_t = exact_dot(inv1, inv0, NN)
    f_t = exact_dot(inv1, exact_dot(alpha1, inv0, TN), NN)
    g_t = exact_dot(upper1, inv0, NN)
    y_w = exact_dot(yy, f_t, NT) + exact_dot(yn, g_t, NT)
    n_w = exact_dot(yy, e_t, NT) - exact_dot(ny, f_t, NT) - exact_dot(nn, g_t, NT)
    known = exact_dot(e_t, y_w, NN) + exact_dot(f_t, n_w, NN)
    coef_ref[0] = alpha1
    coef_ref[1] = upper1.T

    base = exact_dot(e_t, wide_y, NN) - exact_dot(f_t, wide_n, NN)
    rest = exact_dot(f_t, wide_y, NN) + exact_dot(g_t, wide_n, NN)

    wait(SUM2)
    final = send2[0]
    for t in range(1, COLS):
        final = final + got2[t]
    image = exact_dot(e_t, side(final), NN) - rest
    for a in range(3):
        basis_ref[8 * a : 8 * a + 8] = base[:, WIDTH * a : WIDTH * a + WIDTH]

    wait(CROSS2)
    alpha2 = exact_dot(e_t, exact_dot(planes(all4), e_t, NT), NN) - known
    coef_ref[2] = alpha2
    residual = image - exact_dot(alpha2, base, TN)
    for a in range(3):
        resid_ref[8 * a : 8 * a + 8] = residual[:, WIDTH * a : WIDTH * a + WIDTH]

    for kind in range(len(lands)):
        whole(kind).wait_send()


def local(positions, noise):
    vmem = pl.BlockSpec(memory_space=pltpu.VMEM)
    rows = noise.transpose(1, 0, 2).reshape(24, WIDTH)
    basis, residual, coefficients = pl.pallas_call(
        kernel,
        out_shape=(
            jax.ShapeDtypeStruct((24, WIDTH), F32),
            jax.ShapeDtypeStruct((24, WIDTH), F32),
            jax.ShapeDtypeStruct((3, 8, 8), F32),
        ),
        in_specs=[vmem, vmem],
        out_specs=(vmem, vmem, vmem),
        scratch_shapes=[
            pltpu.VMEM((COLS, 3, WIDTH), F32),
            pltpu.VMEM((COLS, 24, WIDTH), F32),
            pltpu.VMEM((PLANE, 3, WIDTH), F32),
            pltpu.VMEM((PLANE, 16, 128), F32),
            pltpu.VMEM((PLANE, 16, 128), F32),
            pltpu.VMEM((16, 128), F32),
            pltpu.VMEM((PLANE, 16, 128), F32),
            pltpu.VMEM((COLS, 16, 128), F32),
            pltpu.VMEM((COLS, 16, 128), F32),
            pltpu.VMEM((COLS, 16, 128), F32),
            pltpu.VMEM((16, 16), F32),
            pltpu.VMEM((16, 16), F32),
            pltpu.VMEM((PLANE, 16, 16), F32),
            pltpu.VMEM((COLS, 16, 16), F32),
            pltpu.VMEM((8, 8), F32),
            pltpu.VMEM((8, 8), F32),
            pltpu.VMEM((PLANE, 8, 8), F32),
            pltpu.VMEM((COLS, 8, 8), F32),
            pltpu.VMEM((3, NCOL, 128), F32),
            pltpu.VMEM((3, NCOL), F32),
            pltpu.VMEM((3, NPLANE), F32),
            pltpu.VMEM((64, NCOL), BF16),
            pltpu.VMEM((64, NPLANE), BF16),
            pltpu.VMEM((8, NCOL, NPLANE), BF16),
            pltpu.VMEM((24, NCOL), F32),
            pltpu.SemaphoreType.DMA((17,)),
            pltpu.SemaphoreType.DMA((17,)),
        ],
        compiler_params=pltpu.CompilerParams(
            collective_id=0, has_side_effects=True, vmem_limit_bytes=60 * 1024 * 1024
        ),
    )(positions, rows)

    def back(value):
        return value.reshape(3, 8, WIDTH).transpose(1, 0, 2)

    return back(basis), back(residual), coefficients


def solution(mesh):
    return jax.shard_map(
        local,
        mesh=mesh,
        in_specs=(P(None, ("row", "col")), P(None, None, ("row", "col"))),
        out_specs=(P(None, None, ("row", "col")), P(None, None, ("row", "col")), P()),
        check_vma=False,
    )
```

```python
import jax
import jax.numpy as jnp
from jax import lax
from jax.experimental import pallas as pl
from jax.experimental.pallas import tpu as pltpu
from jax.sharding import PartitionSpec as P

F32 = jnp.float32
BF16 = jnp.bfloat16
MESH = pl.DeviceIdType.MESH
HIGHEST = lax.Precision.HIGHEST
NT = (((1,), (1,)), ((), ()))
NN = (((1,), (0,)), ((), ()))
TN = (((0,), (0,)), ((), ()))

COLS = 16
PLANE = 32
WIDTH = 64
NCOL = COLS * WIDTH
HOPS = (0, 1, 2, 1)
FAR_FIRST = sorted(range(1, PLANE), key=lambda j: -(2 * (HOPS[j // 8] + HOPS[j // 2 % 4]) + j % 2))
NPLANE = PLANE * WIDTH
CENTRE = 34.1
CHUNK = 256
BEADS = 32768
SHRINK = 0.5**0.5
UNIT = 0.75 * SHRINK
NEAR = 1.0 / UNIT


def dot(left, right, dims):
    return lax.dot_general(left, right, dims, preferred_element_type=F32)


def exact_dot(left, right, dims):
    return lax.dot_general(left, right, dims, precision=HIGHEST, preferred_element_type=F32)


def split(value):
    high = value.astype(BF16)
    return high, (value - high.astype(F32)).astype(BF16)


def pair_strip(col_pos, plane_pos):
    shift = [c - p for c, p in zip(col_pos, plane_pos)]
    square = jnp.maximum(shift[0] * shift[0] + shift[1] * shift[1] + shift[2] * shift[2], 1e-12)
    inv = lax.rsqrt(square)
    inv2 = inv * inv
    inv3 = inv * inv2
    near = square < 2.0
    iso = jnp.where(near, NEAR - 0.75 * (square * inv), inv + inv3 * (1.0 / 3.0))
    along = jnp.where(near, 0.25 * inv, inv3 - inv3 * inv2)
    return [iso] + [along * s for s in shift]


def lower_factor(matrix):
    row = lax.broadcasted_iota(jnp.int32, (8, 8), 0)
    col = lax.broadcasted_iota(jnp.int32, (8, 8), 1)
    left = matrix
    right = jnp.where(row == col, 1.0, 0.0).astype(F32)
    for j in range(8):
        pivot = 1.0 / left[j : j + 1, j : j + 1]
        ratio = jnp.where(row[:, :1] > j, left[:, j : j + 1] * pivot, 0.0)
        left, right = left - ratio * left[j : j + 1, :], right - ratio * right[j : j + 1, :]
    diagonal = jnp.sum(jnp.where(row == col, left, 0.0), axis=1, keepdims=True)
    scale = lax.rsqrt(diagonal)
    scale = scale * (1.5 - 0.5 * diagonal * scale * scale)
    upper = jnp.where(col >= row, left * scale, 0.0)
    return upper, right * scale


def kernel(
    pos_ref, noise_ref, basis_ref, resid_ref, coef_ref,
    col_pos, col_vec, plane_pos, send1, got1, own_y, plane_vec, send2, got2, col_y,
    gram1, gram2, all1, all2, cross1, cross2, all3, all4,
    wide, col_row, plane_row, xs, ys, pair, image2, sent, came,
):
    row = lax.axis_index("row")
    col = lax.axis_index("col")
    x, y, z, core = row >> 2, row & 3, col >> 1, col & 1
    here = (row, col)

    def plane_peer(j):
        dx, dy, dc = j >> 3, (j >> 1) & 3, j & 1
        there = (((x + dx) & 3) * 4 + ((y + dy) & 3), z * 2 + (core ^ dc))
        back = ((((4 - dx) & 3) * 4 + ((4 - dy) & 3)) << 1) + dc
        return there, back

    def col_peer(t):
        return (row, ((z + t) & 15) * 2 + core), (16 - t) & 15

    def near(target):
        return [(target, 1, 4), (target, 12, 4), (target, 5, 4), (target, 9, 3)]

    lands = near(col_pos) + near(col_vec) + [
        (plane_pos, 1, PLANE - 1),
        (got1, 1, PLANE - 1),
        (plane_vec, 1, PLANE - 1),
        (col_y, 1, COLS - 1),
        (got2, 1, COLS - 1),
        (all1, 1, PLANE - 1),
        (all2, 1, COLS - 1),
        (all3, 1, PLANE - 1),
        (all4, 1, COLS - 1),
    ]
    POS, VEC, PLACE, SUM1, IMAGE, COLY, SUM2, GRAM1, GRAM2, CROSS1, CROSS2 = 0, 4, 8, 9, 10, 11, 12, 13, 14, 15, 16

    def copy(kind, source, target, there):
        return pltpu.make_async_remote_copy(
            src_ref=source, dst_ref=target, send_sem=sent.at[kind], recv_sem=came.at[kind],
            device_id=there, device_id_type=MESH,
        )

    def whole(kind):
        target, first, count = lands[kind]
        block = target.at[pl.ds(first, count)]
        return copy(kind, block, block, here)

    def wait(*kinds):
        for kind in kinds:
            whole(kind).wait_recv()

    def to_plane(kind, source):
        for j in FAR_FIRST:
            there, back = plane_peer(j)
            copy(kind, source, lands[kind][0].at[back], there).start()

    def to_col(kind, source):
        for t in (8, 7, 9, 6, 10, 5, 11, 4, 12, 3, 13, 2, 14, 1, 15):
            there, back = col_peer(t)
            copy(kind, source, lands[kind][0].at[back], there).start()

    def to_near(kind, source):
        for d in (4, 3, 2, 1):
            for side, t in ((0, 16 - d), (1, d)):
                there, back = col_peer(t)
                copy(kind + side, source, lands[kind][0].at[back], there).start()

    def relay(kind):
        target = lands[kind][0]
        wait(kind)
        copy(kind + 2, target.at[pl.ds(1, 4)], target.at[pl.ds(5, 4)], col_peer(12)[0]).start()
        wait(kind + 1)
        copy(kind + 3, target.at[pl.ds(13, 3)], target.at[pl.ds(9, 3)], col_peer(4)[0]).start()

    def each(count, step, start=0):
        def body(j, carry):
            step(j)
            return carry
        lax.fori_loop(start, count, body, 0)

    barrier = pltpu.get_barrier_semaphore()
    for peer, slots in ((col_peer, (4, 12, 3, 13, 2, 14, 1, 15)), (plane_peer, FAR_FIRST)):
        for j in slots:
            pl.semaphore_signal(barrier, inc=1, device_id=peer(j)[0], device_id_type=MESH)
    pl.semaphore_wait(barrier, PLANE + 7)

    to_near(POS, pos_ref)
    to_plane(PLACE, pos_ref)
    to_near(VEC, noise_ref)
    col_pos[0] = pos_ref[...]
    plane_pos[0] = pos_ref[...]
    col_vec[0] = noise_ref[...]

    relay(POS)
    wait(PLACE)
    for i in range(PLANE // 2):
        plane_row[:, 128 * i : 128 * i + 128] = (jnp.concatenate([plane_pos[2 * i], plane_pos[2 * i + 1]], axis=1) - CENTRE) * SHRINK
    equal = lax.broadcasted_iota(jnp.int32, (128, 128), 0) == lax.broadcasted_iota(jnp.int32, (128, 128), 1)

    def lanes_of(at):
        return pl.ds(pl.multiple_of(at * CHUNK, CHUNK), CHUNK)

    def plane_of(at):
        here = plane_row[:, lanes_of(at)]
        return [jnp.broadcast_to(here[a : a + 1], (16, CHUNK)) for a in range(3)]

    def build(i, at, plane):
        for k in range(8):
            rows = pl.ds(pl.multiple_of(i * 128 + k * 16, 16), 16)
            column = [jnp.concatenate([wide[a, rows, :]] * (CHUNK // 128), axis=1) for a in range(3)]
            for n, value in enumerate(pair_strip(column, plane)):
                top, rest = split(value)
                pair[2 * n, rows, lanes_of(at)] = top
                pair[2 * n + 1, rows, lanes_of(at)] = rest

    last = NPLANE // CHUNK - 1

    def prepare(i):
        lanes = pl.ds(pl.multiple_of(i * 128, 128), 128)
        both = (jnp.concatenate([col_pos[2 * i], col_pos[2 * i + 1]], axis=1) - CENTRE) * SHRINK
        col_row[:, lanes] = both
        for a in range(3):
            spread = jnp.sum(jnp.where(equal, both[a : a + 1], 0.0), axis=1, keepdims=True)
            wide[a, lanes, :] = jnp.broadcast_to(spread, (128, 128))

    plane = plane_of(last)

    def first(k):
        i = k + (k >> 1) * 4
        prepare(i)
        build(i, last, plane)

    def second(k):
        prepare(k)
        build(k, last, plane)

    each(4, first)
    relay(VEC)
    wait(POS + 2, POS + 3)
    each(6, second, 2)

    def build_all(at):
        plane = plane_of(at)
        each(8, lambda i: build(i, at, plane))

    each(4, lambda step: build_all(last - step), 1)

    def fill(store, vec, lanes, pos):
        along = pos[0:1] * vec[0:8] + pos[1:2] * vec[8:16] + pos[2:3] * vec[16:24]
        top, rest = split(jnp.concatenate([vec, along], axis=0))
        store[0:32, lanes] = top
        store[32:64, lanes] = rest

    wait(VEC + 2, VEC + 3)
    for i in range(COLS // 2):
        lanes = pl.ds(128 * i, 128)
        vec = jnp.concatenate([col_vec[2 * i], col_vec[2 * i + 1]], axis=1)
        fill(xs, vec, lanes, col_row[:, lanes])

    def pack(value, lane):
        x, y, z = (value[8 * a : 8 * a + 8, lane : lane + WIDTH] for a in range(3))
        return jnp.concatenate([x, y], axis=1), jnp.concatenate([z, jnp.zeros_like(z)], axis=1)

    def unpack(one, two):
        return jnp.concatenate([
            jnp.concatenate([one[0:8, 0:WIDTH], two[0:8, 0:WIDTH]], axis=1),
            jnp.concatenate([one[0:8, WIDTH:], two[0:8, WIDTH:]], axis=1),
            jnp.concatenate([one[8:16, 0:WIDTH], two[8:16, 0:WIDTH]], axis=1),
        ], axis=0)

    def finish(at):
        here = plane_row[:, lanes_of(at)]
        full = []
        for n in range(4):
            both = dot(xs[...], pair[2 * n, :, lanes_of(at)], NN)
            full.append(both[0:32] + both[32:64] + dot(xs[0:32, :], pair[2 * n + 1, :, lanes_of(at)], NN))
        image = []
        for a in range(3):
            e = full[1 + a]
            image.append(
                full[0][8 * a : 8 * a + 8] + e[24:32]
                - here[0:1] * e[0:8] - here[1:2] * e[8:16] - here[2:3] * e[16:24]
            )
        image = jnp.concatenate(image, axis=0) * UNIT
        for i in range(CHUNK // WIDTH):
            top, rest = pack(image, WIDTH * i)
            send1[at * (CHUNK // WIDTH) + i, 0:8] = top
            send1[at * (CHUNK // WIDTH) + i, 8:16] = rest

        for i in range(CHUNK // WIDTH):
            j = at * (CHUNK // WIDTH) + i

            @pl.when(j > 0)
            def _():
                there, back = plane_peer(j)
                copy(SUM1, send1.at[j], got1.at[back], there).start()

    each(4, lambda step: finish(last - step))

    def chunk(step):
        at = last - step
        build_all(at)
        finish(at)

    each(NPLANE // CHUNK, chunk, 4)

    wait(SUM1)
    total = send1[0]
    for j in range(1, PLANE):
        total = total + got1[j]
    own_y[...] = total
    to_plane(IMAGE, own_y)
    to_col(COLY, own_y)
    plane_vec[0] = total
    col_y[0] = total

    def side(value):
        return jnp.concatenate([value[0:8], value[8:16, 0:WIDTH]], axis=1)

    vec_n = noise_ref[...]
    wide_n = jnp.concatenate([vec_n[0:8], vec_n[8:16], vec_n[16:24]], axis=1)
    wide_y = side(total)
    block = jnp.concatenate([wide_n, wide_y], axis=0)
    gram = exact_dot(block, block, NT)
    gram1[...] = gram
    to_plane(GRAM1, gram1)
    all1[0] = gram

    wait(IMAGE)
    for i in range(PLANE // 2):
        lanes = pl.ds(128 * i, 128)
        fill(ys, unpack(plane_vec[2 * i], plane_vec[2 * i + 1]), lanes, plane_row[:, lanes])

    def tile(at):
        rows = lanes_of(at)
        here = col_row[:, rows]
        full = []
        for n in range(4):
            both = dot(ys[...], pair[2 * n, rows, :], NT)
            full.append(both[0:32] + both[32:64])
        image = []
        for a in range(3):
            e = full[1 + a]
            image.append(
                full[0][8 * a : 8 * a + 8] - e[24:32]
                + here[0:1] * e[0:8] + here[1:2] * e[8:16] + here[2:3] * e[16:24]
            )
        image = jnp.concatenate(image, axis=0) * UNIT
        image2[:, rows] = image
        for i in range(CHUNK // WIDTH):
            top, rest = pack(image, WIDTH * i)
            send2[at * (CHUNK // WIDTH) + i, 0:8] = top
            send2[at * (CHUNK // WIDTH) + i, 8:16] = rest

        for i in range(CHUNK // WIDTH):
            t = at * (CHUNK // WIDTH) + i

            @pl.when(t > 0)
            def _():
                there, back = col_peer(t)
                copy(SUM2, send2.at[t], got2.at[back], there).start()

    each(NCOL // CHUNK, tile)

    wait(COLY)
    cross = jnp.zeros((8, 8), F32)
    y_rows = jnp.concatenate([unpack(col_y[t], col_y[t + 1]) for t in range(0, COLS, 2)], axis=1)
    for a in range(3):
        part = slice(8 * a, 8 * a + 8)
        cross = cross + exact_dot(y_rows[part], image2[part, :], NT)
    cross1[...] = cross
    to_plane(CROSS1, cross1)
    all3[0] = cross

    wait(GRAM1)
    for j in range(1, PLANE):
        gram = gram + all1[j]
    gram2[...] = gram
    to_col(GRAM2, gram2)
    all2[0] = gram

    wait(CROSS1)
    for j in range(1, PLANE):
        cross = cross + all3[j]
    cross2[...] = cross
    to_col(CROSS2, cross2)
    all4[0] = cross

    def planes(store):
        value = store[(16 - z) % 16]
        for t in range(1, COLS):
            value = value + store[(t + 16 - z) % 16]
        return value * (1.0 / (3.0 * BEADS))

    wait(GRAM2)
    gram = planes(all2)
    nn, ny, yn, yy = gram[0:8, 0:8], gram[0:8, 8:16], gram[8:16, 0:8], gram[8:16, 8:16]
    upper0, inv0 = lower_factor(nn)
    alpha1 = exact_dot(exact_dot(inv0, ny, NN), inv0, NT)
    image_gram = exact_dot(exact_dot(inv0, yy, NN), inv0, NT)
    upper1, inv1 = lower_factor(image_gram - exact_dot(alpha1, alpha1, TN))
    e_t = exact_dot(inv1, inv0, NN)
    f_t = exact_dot(inv1, exact_dot(alpha1, inv0, TN), NN)
    g_t = exact_dot(upper1, inv0, NN)
    y_w = exact_dot(yy, f_t, NT) + exact_dot(yn, g_t, NT)
    n_w = exact_dot(yy, e_t, NT) - exact_dot(ny, f_t, NT) - exact_dot(nn, g_t, NT)
    known = exact_dot(e_t, y_w, NN) + exact_dot(f_t, n_w, NN)
    coef_ref[0] = alpha1
    coef_ref[1] = upper1.T

    base = exact_dot(e_t, wide_y, NN) - exact_dot(f_t, wide_n, NN)
    rest = exact_dot(f_t, wide_y, NN) + exact_dot(g_t, wide_n, NN)

    wait(SUM2)
    final = send2[0]
    for t in range(1, COLS):
        final = final + got2[t]
    image = exact_dot(e_t, side(final), NN) - rest
    for a in range(3):
        basis_ref[8 * a : 8 * a + 8] = base[:, WIDTH * a : WIDTH * a + WIDTH]

    wait(CROSS2)
    alpha2 = exact_dot(e_t, exact_dot(planes(all4), e_t, NT), NN) - known
    coef_ref[2] = alpha2
    residual = image - exact_dot(alpha2, base, TN)
    for a in range(3):
        resid_ref[8 * a : 8 * a + 8] = residual[:, WIDTH * a : WIDTH * a + WIDTH]

    for kind in range(len(lands)):
        whole(kind).wait_send()


def local(positions, noise):
    vmem = pl.BlockSpec(memory_space=pltpu.VMEM)
    rows = noise.transpose(1, 0, 2).reshape(24, WIDTH)
    basis, residual, coefficients = pl.pallas_call(
        kernel,
        out_shape=(
            jax.ShapeDtypeStruct((24, WIDTH), F32),
            jax.ShapeDtypeStruct((24, WIDTH), F32),
            jax.ShapeDtypeStruct((3, 8, 8), F32),
        ),
        in_specs=[vmem, vmem],
        out_specs=(vmem, vmem, vmem),
        scratch_shapes=[
            pltpu.VMEM((COLS, 3, WIDTH), F32),
            pltpu.VMEM((COLS, 24, WIDTH), F32),
            pltpu.VMEM((PLANE, 3, WIDTH), F32),
            pltpu.VMEM((PLANE, 16, 128), F32),
            pltpu.VMEM((PLANE, 16, 128), F32),
            pltpu.VMEM((16, 128), F32),
            pltpu.VMEM((PLANE, 16, 128), F32),
            pltpu.VMEM((COLS, 16, 128), F32),
            pltpu.VMEM((COLS, 16, 128), F32),
            pltpu.VMEM((COLS, 16, 128), F32),
            pltpu.VMEM((16, 16), F32),
            pltpu.VMEM((16, 16), F32),
            pltpu.VMEM((PLANE, 16, 16), F32),
            pltpu.VMEM((COLS, 16, 16), F32),
            pltpu.VMEM((8, 8), F32),
            pltpu.VMEM((8, 8), F32),
            pltpu.VMEM((PLANE, 8, 8), F32),
            pltpu.VMEM((COLS, 8, 8), F32),
            pltpu.VMEM((3, NCOL, 128), F32),
            pltpu.VMEM((3, NCOL), F32),
            pltpu.VMEM((3, NPLANE), F32),
            pltpu.VMEM((64, NCOL), BF16),
            pltpu.VMEM((64, NPLANE), BF16),
            pltpu.VMEM((8, NCOL, NPLANE), BF16),
            pltpu.VMEM((24, NCOL), F32),
            pltpu.SemaphoreType.DMA((17,)),
            pltpu.SemaphoreType.DMA((17,)),
        ],
        compiler_params=pltpu.CompilerParams(
            collective_id=0, has_side_effects=True, vmem_limit_bytes=60 * 1024 * 1024
        ),
    )(positions, rows)

    def back(value):
        return value.reshape(3, 8, WIDTH).transpose(1, 0, 2)

    return back(basis), back(residual), coefficients


def solution(mesh):
    return jax.shard_map(
        local,
        mesh=mesh,
        in_specs=(P(None, ("row", "col")), P(None, None, ("row", "col"))),
        out_specs=(P(None, None, ("row", "col")), P(None, None, ("row", "col")), P()),
        check_vma=False,
    )
```
